32 devices in a mesh: axial: 4 (over z), azim: 8 (over y, x, core).
Axes of the slice: x: 2, y: 2, z: 4, core: 2. Of those that a mesh axis runs over, the one named last changes fastest.
Arguments:
- fields: float32 [4096, 4, 1024], P(('axial', 'azim')), may hold values from -6 to 6
- new_owner: int32 [4096, 1], P(('axial', 'azim')), may hold values from 0 to 31; in each aligned block of 128 rows (0 to 127, 128 to 255, ...) at most 6 rows name the same one
- leaflet: bfloat16 [64, 128, 2048], P(None, 'axial', 'azim'), may hold values from -6 to 6
- stiffness: bfloat16 [64, 64], replicated, may hold values from -0.75 to 0.75
- coarse: float32 [2048, 256], P(('axial', 'azim')), may hold values from -6 to 6
- coarse_of_slot: int32 [6144], P(('axial', 'azim')), may hold values from 0 to 63
- viscosity: float32 [4], replicated, may hold values from 0.02 to 0.2
Outputs:
- regridded: float32 [6144, 4, 1024], P(('axial', 'azim'))
The draws below stay inside these ranges and needn't reach their ends.
Inputs may be any that keep to these rules, and one draw needn't show every extreme that they name: `new_owner`: among the patches of one device, at most 6 share a new owner; in some device's patches exactly 6 do.
All inputs are finite; a program needn't handle non-finite values.
Results may differ from the reference program's by a relative error of at most 0.004.
Values may be sent and summed in bfloat16 or wider, within the bound.
A program may use at most 64 MiB of HBM per device.

```python
import math
import jax
import jax.numpy as jnp
import numpy as np
from jax import lax

PR = 16
PC = 64
FIELDS = 4
REC = 64
ZP = 4
CC = 64
STEPS = 2
P_DEV = 128
SC = 6
RS = 192
P_TOTAL = 4096
NA_DEV = 32
NZ_DEV = 256
N_AXIAL = 4
N_AZIM = 8
DEVICES = 32


def plant(values, own_key, low, high):
    extent = values.shape
    index_at = [jax.random.randint(jax.random.fold_in(own_key, axis), (), 0, extent[axis]) for axis in range(len(extent))]
    values = values.at[tuple(index_at)].set(low)
    longest = extent.index(max(extent))
    index_at[longest] = (index_at[longest] + 1) % extent[longest]
    return values.at[tuple(index_at)].set(high)


def block_levels(rng, dims, pieces, smallest, largest):
    def one(dim, parts):
        steps = jax.random.uniform(jax.random.fold_in(jax.random.fold_in(rng, 6), dim), (parts,), jnp.float32, smallest / len(pieces), largest / len(pieces))
        return jnp.repeat(jnp.exp(steps), dims[dim] // parts).reshape((-1,) + (1,) * (len(dims) - dim - 1))

    level = one(*pieces[0])
    for cut in pieces[1:]:
        level = level * one(*cut)
    return level


def routed_block(key, own, number, rows, count, top, most, lean):
    ranking = jax.random.permutation(key, count)
    heavy_load, common = shares(count, rows * top, most, lean, True), shares(count, rows * top, most, lean, False)
    places = jnp.arange(count)

    def named(sizes, turn):
        used = int((sizes > 0).sum())
        fixed = max(1, used // 4)
        passed = fixed + (places - fixed + turn * (used - fixed)) % max(1, count - fixed)
        return jnp.zeros((count,), jnp.int32).at[ranking[jnp.where(places < fixed, places, passed)]].set(jnp.asarray(sizes, jnp.int32))

    sizes = jnp.where(number % 4 == 0, named(heavy_load, number // 4), named(common, number - number // 4 - 1))
    mixed = jax.random.permutation(jax.random.fold_in(own, 3), count)
    giver, taker = mixed[0:count // 2 * 2:2], mixed[1:count // 2 * 2:2]
    margin = jnp.minimum(sizes[giver] - 1, most - sizes[taker]) // 2
    margin = jnp.where((giver == ranking[0]) | (taker == ranking[0]) | (sizes[taker] == 0), 0, jnp.maximum(margin, 0))
    passed = jax.random.randint(jax.random.fold_in(own, 4), (count // 2,), 0, 1 << 20) % (margin + 1)
    sizes = sizes.at[giver].add(-passed).at[taker].add(passed)
    items = jnp.searchsorted(jnp.cumsum(sizes), jnp.arange(rows * top), side="right").astype(jnp.int32)
    table = items.reshape(top, rows).T
    table = table[jax.random.permutation(jax.random.fold_in(own, 1), rows)]
    turn = jax.random.randint(jax.random.fold_in(own, 2), (rows, 1), 0, top)
    return jnp.take_along_axis(table, (jnp.arange(top)[None, :] + turn) % top, axis=1)


def shares(amount, total, most, lean, full):
    weights = [(1 << 20) // math.isqrt(standing ** lean) + 1 for standing in range(1, amount + 1)]
    largest = most if full else min(most, max(-(-total // amount), total * weights[0] // sum(weights)))
    least = 1 if total - largest >= amount - 1 else 0
    given, surplus = [largest] + [least] * (amount - 1), total - largest - least * (amount - 1)
    while surplus > 0:
        free = [i for i in range(1, amount) if given[i] < largest] or [i for i in range(1, amount) if given[i] < most]
        mass, budget = sum([weights[i] for i in free]), surplus
        for i in free:
            more = min(most - given[i], max(1, budget * weights[i] // mass), surplus)
            given[i] = given[i] + more
            surplus = surplus - more
    return np.array(given)


def noise(rng, shape, deviation, reach, cuts=(), kind=jnp.bfloat16):
    loudness = block_levels(rng, shape, cuts, -0.22, 0.18) if cuts else 1.0
    entries = jax.random.normal(rng, shape, jnp.float32) * deviation * loudness
    return jnp.minimum(jnp.maximum(entries, -reach), reach).astype(kind)


def setup_inputs(seed: int = 0) -> dict:
    arg_keys = jax.random.split(jax.random.key(seed), 8)
    fields = noise(arg_keys[0], (P_TOTAL, FIELDS, PR * PC), 1.0, 6.0, ((0, 32),), jnp.float32)
    new_owner_keys = jax.random.split(jax.random.fold_in(arg_keys[1], 1), P_TOTAL // P_DEV)
    new_owner_turns = jax.random.permutation(jax.random.fold_in(arg_keys[1], 3), P_TOTAL // P_DEV)
    new_owner = jax.vmap(lambda own, number: routed_block(jax.random.fold_in(arg_keys[1], 2), own, number, P_DEV, DEVICES, 1, SC, 2))(new_owner_keys, new_owner_turns).reshape((P_TOTAL, 1))
    leaflet = noise(arg_keys[2], (REC, NA_DEV * N_AXIAL, NZ_DEV * N_AZIM), 1.0, 6.0, ((1, 4), (2, 8)))
    stiffness = noise(arg_keys[3], (REC, REC), REC ** -0.5, 0.75)
    coarse = noise(arg_keys[4], (DEVICES * CC, FIELDS * PC), 1.0, 6.0, ((0, 32),), jnp.float32)
    coarse_of_slot = plant(jax.random.randint(arg_keys[5], (DEVICES * RS,), 0, CC), jax.random.fold_in(arg_keys[5], 1), 0, CC - 1).astype(jnp.int32)
    viscosity = jnp.clip(jax.random.uniform(arg_keys[6], (FIELDS,), jnp.float32, 0.02, 0.2), 0.02, 0.2)
    return dict(fields=fields, new_owner=new_owner, leaflet=leaflet, stiffness=stiffness, coarse=coarse, coarse_of_slot=coarse_of_slot, viscosity=viscosity)


SPREAD = 0.25


def interp_table(coarse_cols):
    fine_col = jnp.arange(2 * coarse_cols)
    nearest = fine_col // 2
    second = jnp.where(fine_col % 2 == 0, jnp.maximum(nearest - 1, 0), jnp.minimum(nearest + 1, coarse_cols - 1))
    coarse_row = jnp.arange(coarse_cols)[:, None]
    return 0.75 * (coarse_row == nearest[None, :]).astype(jnp.float32) + 0.25 * (coarse_row == second[None, :]).astype(jnp.float32)


def viscous(state, ghosts, viscosity):
    row_pad = jnp.concatenate([ghosts[:, :, 0:1, :], state, ghosts[:, :, 1:2, :]], axis=2)
    col_pad = jnp.pad(state, ((0, 0), (0, 0), (0, 0), (1, 1)))
    laplace = row_pad[:, :, 2:, :] + row_pad[:, :, :-2, :] + col_pad[:, :, :, 2:] + col_pad[:, :, :, :-2] - 4.0 * state
    return state + viscosity[None, :, None, None] * laplace


def reference(fields, new_owner, leaflet, stiffness, coarse, coarse_of_slot, viscosity):
    points = leaflet.astype(jnp.float32)
    padded = jnp.pad(points, ((0, 0), (1, 1), (0, 0)))
    laplace = padded[:, 2:, :] + padded[:, :-2, :] + jnp.roll(points, 1, 2) + jnp.roll(points, -1, 2) - 4.0 * points
    laplace = laplace.astype(jnp.bfloat16)
    tension = jnp.dot(stiffness, laplace.reshape(REC, -1), preferred_element_type=jnp.float32).astype(jnp.bfloat16)
    tension = tension.reshape(REC, N_AXIAL, NA_DEV, N_AZIM, ZP, PC)
    sheets = tension.transpose(1, 3, 2, 4, 0, 5).reshape(P_TOTAL, FIELDS, PR * PC)
    forced = fields + SPREAD * sheets.astype(jnp.float32)

    owners = new_owner.reshape(DEVICES, P_DEV)
    position = jnp.arange(P_DEV)

    def ranks(owner_row):
        earlier = (owner_row[:, None] == owner_row[None, :]) & (position[None, :] < position[:, None])
        return jnp.sum(earlier.astype(jnp.int32), axis=1)

    ranked = lax.map(ranks, owners)
    target = owners * RS + jnp.arange(DEVICES, dtype=jnp.int32)[:, None] * SC + ranked
    placed = jnp.zeros((DEVICES * RS, FIELDS, PR * PC), jnp.float32).at[target.reshape(-1).astype(jnp.int32)].set(forced)

    interp = interp_table(PC // 2)

    def relax(inputs):
        blocks, strips, picked = inputs
        chosen = jnp.take(strips, picked, axis=0).reshape(RS, FIELDS, 2, PC // 2)
        ghosts = jnp.einsum("sfgk,kc->sfgc", chosen, interp, precision=lax.Precision.HIGHEST)
        state = blocks.reshape(RS, FIELDS, PR, PC)
        for sweep in range(STEPS):
            state = viscous(state, ghosts, viscosity)
        return state.reshape(RS, FIELDS, PR * PC)

    result = lax.map(relax, (placed.reshape(DEVICES, RS, FIELDS, PR * PC), coarse.reshape(DEVICES, CC, FIELDS * PC), coarse_of_slot.reshape(DEVICES, RS)))
    return result.reshape(DEVICES * RS, FIELDS, PR * PC)
```

```python
import functools
import jax
import jax.numpy as jnp
from jax import lax
from jax.experimental import pallas as pl
from jax.experimental.pallas import tpu as pltpu
from jax.sharding import PartitionSpec as P

PC = 64
FIELDS = 4
STEPS = 2
SPREAD = 0.25
LANES = 128
MESH = pl.DeviceIdType.MESH
F32 = jnp.float32
BF16 = jnp.bfloat16


def iota(shape, dim):
    return lax.broadcasted_iota(jnp.int32, shape, dim)


def peers(n_ax, n_az):
    half = n_ax // 2
    near = sorted(range(n_ax), key=lambda d: abs(d - half))
    return [(da, dz) for da in near for dz in range(n_az) if (da, dz) != (0, 0)]


def send_kernel(
    n_ax, n_az, each, pick_ref, fields_ref, leaf_ref, stiff_ref, out_ref,
    rows_f, cols_f, edge_rows, edge_cols, got_rows, got_cols, lap_ref, forced_ref, packed_ref,
    halo_send, halo_recv, send_sem, recv_sem,
):
    a = lax.axis_index("axial")
    z = lax.axis_index("azim")
    me = a * n_az + z
    records, rows, cols = leaf_ref.shape
    patches = fields_ref.shape[0]
    blocks = rows // 8
    order = peers(n_ax, n_az)

    got_rows[...] = jnp.zeros_like(got_rows)
    barrier = pltpu.get_barrier_semaphore()
    for da, dz in order:
        pl.semaphore_signal(
            barrier, inc=1,
            device_id=(lax.rem(a + da, n_ax), lax.rem(z + dz, n_az)), device_id_type=MESH,
        )

    row_id = iota((rows, LANES), 0)
    lane_id = iota((rows, LANES), 1)
    eye_low = lane_id == row_id
    eye_high = lane_id == row_id + rows

    def edges(k, carry):
        x = leaf_ref[k].astype(F32)
        rows_f[0, pl.ds(k, 1), :] = x[0:1, :]
        rows_f[1, pl.ds(k, 1), :] = x[rows - 1:rows, :]
        first = jnp.broadcast_to(x[:, 0:1], (rows, LANES))
        last = jnp.broadcast_to(x[:, cols - 1:cols], (rows, LANES))
        both = jnp.where(eye_low, first, jnp.where(eye_high, last, 0.0))
        cols_f[pl.ds(k, 1), :] = jnp.sum(both, axis=0, keepdims=True)
        return carry

    lax.fori_loop(0, records, edges, 0, unroll=4)
    edge_rows[...] = rows_f[...].astype(BF16)
    edge_cols[...] = cols_f[...].astype(BF16)
    pl.semaphore_wait(barrier, len(order))

    def halo(src, dst, i, device):
        return pltpu.make_async_remote_copy(
            src_ref=src, dst_ref=dst, send_sem=halo_send.at[i], recv_sem=halo_recv.at[i],
            device_id=device, device_id_type=MESH,
        )

    down = halo(edge_rows.at[1], got_rows.at[0], 0, (lax.rem(a + 1, n_ax), z))
    up = halo(edge_rows.at[0], got_rows.at[1], 1, (lax.rem(a + n_ax - 1, n_ax), z))
    right = halo(edge_cols, got_cols.at[0], 2, (a, lax.rem(z + 1, n_az)))
    left = halo(edge_cols, got_cols.at[1], 3, (a, lax.rem(z + n_az - 1, n_az)))

    @pl.when(a < n_ax - 1)
    def _():
        down.start()

    @pl.when(a > 0)
    def _():
        up.start()

    right.start()
    left.start()

    pairs = records // FIELDS // 2
    width = pairs * FIELDS
    big = 8 * records
    out_row = iota((big, records), 0)
    record = iota((big, records), 1)
    within = lax.rem(out_row, width)
    wanted = lax.rem(within, FIELDS) * (2 * pairs) + 2 * (within // FIELDS) + out_row // (8 * width)
    row_pick = (record == wanted).astype(BF16)
    col_pick = (iota((records, big), 0) == iota((records, big), 1) // 8).astype(BF16)
    spread = jnp.dot(stiff_ref[...], col_pick, preferred_element_type=F32).astype(BF16)
    spread = jnp.dot(row_pick, spread, preferred_element_type=F32)
    same = lax.rem(iota((big, big), 0) // width, 8) == lax.rem(iota((big, big), 1), 8)
    law = jnp.where(same, spread, 0.0).astype(BF16)
    forced_ref[patches] = jnp.zeros(forced_ref.shape[1:], BF16)

    @pl.when(a > 0)
    def _():
        down.wait_recv()

    @pl.when(a < n_ax - 1)
    def _():
        up.wait_recv()

    right.wait_recv()
    left.wait_recv()
    rows_f2 = got_rows[...].astype(F32)
    cols_l = got_cols[0].astype(F32)
    cols_r = got_cols[1].astype(F32)

    @pl.when(a < n_ax - 1)
    def _():
        down.wait_send()

    @pl.when(a > 0)
    def _():
        up.wait_send()

    right.wait_send()
    left.wait_send()
    rows_f[...] = rows_f2
    cols_f[...] = jnp.where(iota(cols_l.shape, 1) < rows, cols_r, cols_l)
    wide_row = iota((rows, cols), 0)
    wide_lane = iota((rows, cols), 1)

    def laplace(k, carry):
        x = leaf_ref[k].astype(F32)
        halo_cols = jnp.broadcast_to(cols_f[pl.ds(k, 1), :], (rows, LANES))
        after = jnp.sum(jnp.where(eye_low, halo_cols, 0.0), axis=1, keepdims=True)
        before = jnp.sum(jnp.where(eye_high, halo_cols, 0.0), axis=1, keepdims=True)
        north = jnp.where(wide_row == 0, rows_f[0, pl.ds(k, 1), :], pltpu.roll(x, 1, 0))
        south = jnp.where(wide_row == rows - 1, rows_f[1, pl.ds(k, 1), :], pltpu.roll(x, rows - 1, 0))
        west = jnp.where(wide_lane == 0, before, pltpu.roll(x, 1, 1))
        east = jnp.where(wide_lane == cols - 1, after, pltpu.roll(x, cols - 1, 1))
        total = south + north + west + east - 4.0 * x
        for b in range(blocks):
            lap_ref[b, pl.ds(pl.multiple_of(k * 8, 8), 8), :] = total[b * 8:(b + 1) * 8, :]
        return carry

    lax.fori_loop(0, records, laplace, 0, unroll=4)

    low = iota((width, LANES), 1) < PC
    across = cols // PC

    def force(b, carry):
        tension = jnp.dot(law, lap_ref[b].astype(BF16), preferred_element_type=F32)
        tension = tension.astype(BF16).astype(F32) * SPREAD
        for r in range(8):
            for t in range(cols // LANES):
                even = tension[r * width:(r + 1) * width, t * LANES:(t + 1) * LANES]
                odd = tension[(8 + r) * width:(9 + r) * width, t * LANES:(t + 1) * LANES]
                p = (b * 8 + r) * across + 2 * t
                first = jnp.where(low, even, pltpu.roll(odd, PC, 1))
                second = jnp.where(low, pltpu.roll(even, PC, 1), odd)
                forced_ref[p] = (fields_ref[p] + first).astype(BF16)
                forced_ref[p + 1] = (fields_ref[p + 1] + second).astype(BF16)
        return carry

    lax.fori_loop(0, blocks, force, 0)

    copies = []
    for i, (da, dz) in enumerate(order):
        ta, tz = lax.rem(a + da, n_ax), lax.rem(z + dz, n_az)
        other = ta * n_az + tz
        for k in range(each):
            packed_ref[other, k] = forced_ref[pick_ref[other * each + k]]
        copy = pltpu.make_async_remote_copy(
            src_ref=packed_ref.at[other], dst_ref=out_ref.at[me],
            send_sem=send_sem.at[i], recv_sem=recv_sem.at[i],
            device_id=(ta, tz), device_id_type=MESH,
        )
        copy.start()
        copies.append(copy)
    for k in range(each):
        out_ref[me, k] = forced_ref[pick_ref[me * each + k]]
    for i, (da, dz) in enumerate(order):
        source = lax.rem(a + n_ax - da, n_ax) * n_az + lax.rem(z + n_az - dz, n_az)
        pltpu.make_async_remote_copy(
            src_ref=packed_ref.at[source], dst_ref=out_ref.at[source],
            send_sem=send_sem.at[i], recv_sem=recv_sem.at[i],
            device_id=(a, z), device_id_type=MESH,
        ).wait_recv()
    for copy in copies:
        copy.wait_send()


def step_slots(state, ghost, nu):
    slots, height, lanes = state.shape
    shape = (slots, height, lanes)
    lane = iota(shape, 2)
    row = iota(shape, 1)
    cell = lax.rem(lane, PC)
    flat = slots * height
    for _ in range(STEPS):
        wide = state.reshape(flat, lanes)
        swap = pltpu.roll(wide, PC, 1).reshape(shape)
        west = jnp.where(cell == 0, 0.0, pltpu.roll(wide, 1, 1).reshape(shape))
        east = jnp.where(cell == PC - 1, 0.0, pltpu.roll(wide, lanes - 1, 1).reshape(shape))
        above = jnp.concatenate([ghost, swap[:, :height - FIELDS]], axis=1)
        below = jnp.concatenate([swap[:, FIELDS:], ghost], axis=1)
        total = swap + jnp.where(lane < PC, above, below) + west + east - 4.0 * state
        state = state + nu * total
    return state


def relax_kernel(group, idx_ref, coarse_ref, nu_ref, in_ref, out_ref, ghost_ref):
    @pl.when(pl.program_id(0) == 0)
    def _():
        strips = coarse_ref.shape[0]
        fine = iota((PC, LANES), 1)
        src = iota((PC, LANES), 0)
        half = PC // 2
        near = (fine // PC) * half + lax.rem(fine, PC) // 2
        cell = lax.rem(fine, PC)
        second = jnp.where(
            lax.rem(fine, 2) == 0,
            jnp.where(cell == 0, near, near - 1),
            jnp.where(cell == PC - 1, near, near + 1),
        )
        table = (0.75 * (src == near).astype(F32) + 0.25 * (src == second).astype(F32)).astype(BF16)
        hot = (idx_ref[...] == iota((idx_ref.shape[0], FIELDS * strips), 1)).astype(BF16)
        parts = []
        for f in range(FIELDS):
            raw = coarse_ref[:, f * PC:(f + 1) * PC]
            top = raw.astype(BF16)
            rest = (raw - top.astype(F32)).astype(BF16)
            parts.append(
                jnp.dot(top, table, preferred_element_type=F32)
                + jnp.dot(rest, table, preferred_element_type=F32)
            )
        strip = jnp.concatenate(parts, axis=0)
        top = strip.astype(BF16)
        rest = (strip - top.astype(F32)).astype(BF16)
        ghost = jnp.dot(hot, top, preferred_element_type=F32)
        ghost = ghost + jnp.dot(hot, rest, preferred_element_type=F32)
        ghost_ref[...] = ghost.reshape(ghost_ref.shape)

    base = pl.program_id(0) * group
    for s in range(group):
        ghost = ghost_ref[base + s][None, :FIELDS]
        out_ref[s] = step_slots(in_ref[s].astype(F32)[None], ghost, nu_ref[...][None])[0]


def shards(mesh, fields, new_owner, leaflet, stiffness, coarse, coarse_of_slot, viscosity):
    n_ax, n_az = mesh.shape["axial"], mesh.shape["azim"]
    devices = n_ax * n_az
    patches, _, section = fields.shape
    records = leaflet.shape[0]
    each = max(2, 3 * patches // (2 * devices))
    slots = devices * each
    owners = new_owner[:, 0]
    place = jnp.arange(patches)
    earlier = (owners[:, None] == owners[None, :]) & (place[None, :] < place[:, None])
    target = owners * each + jnp.sum(earlier.astype(jnp.int32), axis=1)
    taken = target[None, :] == jnp.arange(slots)[:, None]
    pick = patches + jnp.sum(jnp.where(taken, place[None, :] - patches, 0), axis=1)
    height = FIELDS * section // LANES
    view = fields.reshape(patches, FIELDS, section // LANES, LANES).transpose(0, 2, 1, 3)
    view = view.reshape(patches, height, LANES)
    rows, cols = leaflet.shape[1:]
    vmem = pl.BlockSpec(memory_space=pltpu.VMEM)
    moved = pl.pallas_call(
        functools.partial(send_kernel, n_ax, n_az, each),
        out_shape=jax.ShapeDtypeStruct((devices, each, height, LANES), BF16),
        in_specs=[pl.BlockSpec(memory_space=pltpu.SMEM), vmem, vmem, vmem],
        out_specs=vmem,
        scratch_shapes=[
            pltpu.VMEM((2, records, cols), F32),
            pltpu.VMEM((records, LANES), F32),
            pltpu.VMEM((2, records, cols), BF16),
            pltpu.VMEM((records, LANES), BF16),
            pltpu.VMEM((2, records, cols), BF16),
            pltpu.VMEM((2, records, LANES), BF16),
            pltpu.VMEM((rows // 8, 8 * records, cols), F32),
            pltpu.VMEM((patches + 1, height, LANES), BF16),
            pltpu.VMEM((devices, each, height, LANES), BF16),
            pltpu.SemaphoreType.DMA((4,)),
            pltpu.SemaphoreType.DMA((4,)),
            pltpu.SemaphoreType.DMA((devices - 1,)),
            pltpu.SemaphoreType.DMA((devices - 1,)),
        ],
        compiler_params=pltpu.CompilerParams(collective_id=0, has_side_effects=True),
        name="send",
    )(pick, view, leaflet, stiffness)

    group = 16
    index = coarse_of_slot[:, None] + coarse.shape[0] * (jnp.arange(2 * FIELDS) % FIELDS)[None, :]
    nu = jnp.broadcast_to(jnp.tile(viscosity, height // FIELDS)[:, None], (height, LANES))
    whole = lambda shape: pl.BlockSpec(shape, lambda i: (0,) * len(shape))
    out = pl.pallas_call(
        functools.partial(relax_kernel, group),
        grid=(slots // group,),
        out_shape=jax.ShapeDtypeStruct((slots, height, LANES), F32),
        in_specs=[
            whole((slots * 2 * FIELDS, 1)), whole(coarse.shape), whole((height, LANES)),
            pl.BlockSpec((group, height, LANES), lambda i: (i, 0, 0)),
        ],
        out_specs=pl.BlockSpec((group, height, LANES), lambda i: (i, 0, 0)),
        scratch_shapes=[pltpu.VMEM((slots, 2 * FIELDS, LANES), F32)],
        name="relax",
    )(index.reshape(-1, 1), coarse, nu, moved.reshape(slots, height, LANES))
    out = out.reshape(slots, section // LANES, FIELDS, LANES).transpose(0, 2, 1, 3)
    return out.reshape(slots, FIELDS, section)


def solution(mesh):
    placed = (
        P(("axial", "azim"), None, None),
        P(("axial", "azim"), None),
        P(None, "axial", "azim"),
        P(),
        P(("axial", "azim"), None),
        P(("axial", "azim")),
        P(),
    )
    return jax.shard_map(
        functools.partial(shards, mesh),
        mesh=mesh,
        in_specs=placed,
        out_specs=P(("axial", "azim"), None, None),
        check_vma=False,
    )
```

```python
import functools
import jax
import jax.numpy as jnp
from jax import lax
from jax.experimental import pallas as pl
from jax.experimental.pallas import tpu as pltpu
from jax.sharding import PartitionSpec as P

PC = 64
FIELDS = 4
STEPS = 2
SPREAD = 0.25
LANES = 128
MESH = pl.DeviceIdType.MESH
F32 = jnp.float32
BF16 = jnp.bfloat16


def iota(shape, dim):
    return lax.broadcasted_iota(jnp.int32, shape, dim)


def peer(i, n_ax, n_az):
    j = i // n_az
    da = lax.rem(n_ax // 2 + ((j + 1) // 2) * (1 - 2 * lax.rem(j, 2)), n_ax)
    return da, lax.rem(lax.rem(i, n_az) + 1, n_az)


def send_kernel(
    n_ax, n_az, each, owner_ref, slot_ref, nu_ref, fields_ref, leaf_ref, stiff_ref, coarse_ref, out_ref,
    rows_f, cols_f, edge_rows, edge_cols, got_rows, got_cols, lap_ref, forced_ref, packed_ref,
    landed_ref, done_ref, strip_ref, pick_row, pick_ref,
    halo_send, halo_recv, send_sem, recv_sem, out_sem, pick_sem,
):
    a = lax.axis_index("axial")
    z = lax.axis_index("azim")
    me = a * n_az + z
    devices = n_ax * n_az
    records, rows, cols = leaf_ref.shape
    patches, height, _ = fields_ref.shape
    blocks = rows // 8

    got_rows[...] = jnp.zeros_like(got_rows)
    barrier = pltpu.get_barrier_semaphore()

    def greet(i, carry):
        da, dz = peer(i, n_ax, n_az)
        pl.semaphore_signal(
            barrier, inc=1,
            device_id=(lax.rem(a + da, n_ax), lax.rem(z + dz, n_az)), device_id_type=MESH,
        )
        return carry

    lax.fori_loop(0, devices - 1, greet, 0)

    row_id = iota((rows, LANES), 0)
    lane_id = iota((rows, LANES), 1)
    eye_low = lane_id == row_id
    eye_high = lane_id == row_id + rows

    def edges(k, carry):
        x = leaf_ref[k].astype(F32)
        rows_f[0, pl.ds(k, 1), :] = x[0:1, :]
        rows_f[1, pl.ds(k, 1), :] = x[rows - 1:rows, :]
        first = jnp.broadcast_to(x[:, 0:1], (rows, LANES))
        last = jnp.broadcast_to(x[:, cols - 1:cols], (rows, LANES))
        both = jnp.where(eye_low, first, jnp.where(eye_high, last, 0.0))
        cols_f[pl.ds(k, 1), :] = jnp.sum(both, axis=0, keepdims=True)
        return carry

    lax.fori_loop(0, records, edges, 0, unroll=4)
    edge_rows[...] = rows_f[...].astype(BF16)
    edge_cols[...] = cols_f[...].astype(BF16)
    pl.semaphore_wait(barrier, devices - 1)

    def halo(src, dst, i, device):
        return pltpu.make_async_remote_copy(
            src_ref=src, dst_ref=dst, send_sem=halo_send.at[i], recv_sem=halo_recv.at[i],
            device_id=device, device_id_type=MESH,
        )

    down = halo(edge_rows.at[1], got_rows.at[0], 0, (lax.rem(a + 1, n_ax), z))
    up = halo(edge_rows.at[0], got_rows.at[1], 1, (lax.rem(a + n_ax - 1, n_ax), z))
    right = halo(edge_cols, got_cols.at[0], 2, (a, lax.rem(z + 1, n_az)))
    left = halo(edge_cols, got_cols.at[1], 3, (a, lax.rem(z + n_az - 1, n_az)))

    @pl.when(a < n_ax - 1)
    def _():
        down.start()

    @pl.when(a > 0)
    def _():
        up.start()

    right.start()
    left.start()

    pairs = records // FIELDS // 2
    width = pairs * FIELDS
    big = 8 * records
    out_row = iota((big, records), 0)
    record = iota((big, records), 1)
    within = lax.rem(out_row, width)
    wanted = lax.rem(within, FIELDS) * (2 * pairs) + 2 * (within // FIELDS) + out_row // (8 * width)
    row_pick = (record == wanted).astype(BF16)
    col_pick = (iota((records, big), 0) == iota((records, big), 1) // 8).astype(BF16)
    spread = jnp.dot(stiff_ref[...], col_pick, preferred_element_type=F32).astype(BF16)
    spread = jnp.dot(row_pick, spread, preferred_element_type=F32)
    same = lax.rem(iota((big, big), 0) // width, 8) == lax.rem(iota((big, big), 1), 8)
    law = jnp.where(same, spread, 0.0).astype(BF16)
    forced_ref[patches] = jnp.zeros(forced_ref.shape[1:], BF16)
    pick_slots(each, owner_ref, pick_row)
    picked = pltpu.make_async_copy(pick_row, pick_ref, pick_sem)
    picked.start()
    interpolate(coarse_ref, strip_ref)

    @pl.when(a > 0)
    def _():
        down.wait_recv()

    @pl.when(a < n_ax - 1)
    def _():
        up.wait_recv()

    right.wait_recv()
    left.wait_recv()
    rows_f2 = got_rows[...].astype(F32)
    cols_l = got_cols[0].astype(F32)
    cols_r = got_cols[1].astype(F32)

    @pl.when(a < n_ax - 1)
    def _():
        down.wait_send()

    @pl.when(a > 0)
    def _():
        up.wait_send()

    right.wait_send()
    left.wait_send()
    rows_f[...] = rows_f2
    cols_f[...] = jnp.where(iota(cols_l.shape, 1) < rows, cols_r, cols_l)
    wide_row = iota((rows, cols), 0)
    wide_lane = iota((rows, cols), 1)

    def laplace(k, carry):
        x = leaf_ref[k].astype(F32)
        halo_cols = jnp.broadcast_to(cols_f[pl.ds(k, 1), :], (rows, LANES))
        after = jnp.sum(jnp.where(eye_low, halo_cols, 0.0), axis=1, keepdims=True)
        before = jnp.sum(jnp.where(eye_high, halo_cols, 0.0), axis=1, keepdims=True)
        north = jnp.where(wide_row == 0, rows_f[0, pl.ds(k, 1), :], pltpu.roll(x, 1, 0))
        south = jnp.where(wide_row == rows - 1, rows_f[1, pl.ds(k, 1), :], pltpu.roll(x, rows - 1, 0))
        west = jnp.where(wide_lane == 0, before, pltpu.roll(x, 1, 1))
        east = jnp.where(wide_lane == cols - 1, after, pltpu.roll(x, cols - 1, 1))
        total = south + north + west + east - 4.0 * x
        for b in range(blocks):
            lap_ref[b, pl.ds(pl.multiple_of(k * 8, 8), 8), :] = total[b * 8:(b + 1) * 8, :]
        return carry

    lax.fori_loop(0, records, laplace, 0, unroll=4)

    low = iota((width, LANES), 1) < PC
    across = cols // PC

    def force(b, carry):
        tension = jnp.dot(law, lap_ref[b].astype(BF16), preferred_element_type=F32)
        tension = tension.astype(BF16).astype(F32) * SPREAD
        for r in range(8):
            for t in range(cols // LANES):
                even = tension[r * width:(r + 1) * width, t * LANES:(t + 1) * LANES]
                odd = tension[(8 + r) * width:(9 + r) * width, t * LANES:(t + 1) * LANES]
                p = (b * 8 + r) * across + 2 * t
                first = jnp.where(low, even, pltpu.roll(odd, PC, 1))
                second = jnp.where(low, pltpu.roll(even, PC, 1), odd)
                forced_ref[p] = (fields_ref[p] + first).astype(BF16)
                forced_ref[p + 1] = (fields_ref[p + 1] + second).astype(BF16)
        return carry

    lax.fori_loop(0, blocks, force, 0)

    picked.wait()

    def outgoing(i):
        da, dz = peer(i, n_ax, n_az)
        ta, tz = lax.rem(a + da, n_ax), lax.rem(z + dz, n_az)
        other = ta * n_az + tz
        return other, pltpu.make_async_remote_copy(
            src_ref=packed_ref.at[other], dst_ref=landed_ref.at[me],
            send_sem=send_sem.at[i], recv_sem=recv_sem.at[i],
            device_id=(ta, tz), device_id_type=MESH,
        )

    def send(i, carry):
        other, copy = outgoing(i)
        for k in range(each):
            packed_ref[other, k] = forced_ref[pick_ref[0, other * each + k]]
        copy.start()
        return carry

    lax.fori_loop(0, devices - 1, send, 0)

    row = iota((height, LANES), 0)
    nu = jnp.full((height, LANES), nu_ref[0], F32)
    for f in range(1, FIELDS):
        nu = jnp.where(lax.rem(row, FIELDS) == f, nu_ref[f], nu)

    def written(source):
        return pltpu.make_async_copy(done_ref.at[source], out_ref.at[source], out_sem.at[source])

    for k in range(each):
        ghost = strip_ref[slot_ref[me * each + k]]
        block = forced_ref[pick_ref[0, me * each + k]].astype(F32)
        done_ref[me, k] = relax(block, ghost, nu)
    written(me).start()

    def arrive(i, carry):
        da, dz = peer(i, n_ax, n_az)
        source = lax.rem(a + n_ax - da, n_ax) * n_az + lax.rem(z + n_az - dz, n_az)
        pltpu.make_async_remote_copy(
            src_ref=packed_ref.at[source], dst_ref=landed_ref.at[source],
            send_sem=send_sem.at[i], recv_sem=recv_sem.at[i],
            device_id=(a, z), device_id_type=MESH,
        ).wait_recv()
        for k in range(each):
            ghost = strip_ref[slot_ref[source * each + k]]
            done_ref[source, k] = relax(landed_ref[source, k].astype(F32), ghost, nu)
        written(source).start()
        return carry

    lax.fori_loop(0, devices - 1, arrive, 0)

    def finish(i, carry):
        outgoing(i)[1].wait_send()
        written(i).wait()
        return carry

    lax.fori_loop(0, devices - 1, finish, 0)
    written(devices - 1).wait()


def pick_slots(each, owner_ref, pick_row):
    patches = owner_ref.shape[1]
    slots = pick_row.shape[1]
    square = (patches, patches)
    eye = iota(square, 0) == iota(square, 1)
    owner = owner_ref[...]
    across = jnp.broadcast_to(owner, square)
    along = jnp.sum(jnp.where(eye, across, 0), axis=1, keepdims=True)
    earlier = (along == across) & (iota(square, 0) < iota(square, 1))
    rank = jnp.sum(earlier.astype(jnp.int32), axis=0, keepdims=True)
    target = jnp.broadcast_to(owner * each + rank, square)
    target = jnp.sum(jnp.where(eye, target, 0), axis=1, keepdims=True)
    shape = (patches, slots)
    taken = target == iota(shape, 1)
    pick_row[...] = patches + jnp.sum(
        jnp.where(taken, iota(shape, 0) - patches, 0), axis=0, keepdims=True
    )


def interpolate(coarse_ref, strip_ref):
    fine = iota((PC, LANES), 1)
    src = iota((PC, LANES), 0)
    cell = lax.rem(fine, PC)
    near = (fine // PC) * (PC // 2) + cell // 2
    second = jnp.where(
        lax.rem(fine, 2) == 0,
        jnp.where(cell == 0, near, near - 1),
        jnp.where(cell == PC - 1, near, near + 1),
    )
    table = (0.75 * (src == near).astype(F32) + 0.25 * (src == second).astype(F32)).astype(BF16)
    for f in range(FIELDS):
        raw = coarse_ref[:, f * PC:(f + 1) * PC]
        top = raw.astype(BF16)
        rest = (raw - top.astype(F32)).astype(BF16)
        fine_cells = jnp.dot(top, table, preferred_element_type=F32)
        fine_cells = fine_cells + jnp.dot(rest, table, preferred_element_type=F32)
        strip_ref[:, f, :] = fine_cells
        strip_ref[:, FIELDS + f, :] = fine_cells


def relax(state, ghost, nu):
    shape = (8, LANES)
    lane = iota(shape, 1)
    low = iota(shape, 0) < FIELDS
    cell = lax.rem(lane, PC)
    up = (lane < PC) & low
    down = (lane >= PC) & (iota(shape, 0) >= FIELDS)
    count = state.shape[0] // 8
    tiles = [state[8 * j:8 * j + 8] for j in range(count)]
    for _ in range(STEPS):
        swap = [pltpu.roll(t, PC, 1) for t in tiles]
        turned = [ghost] + [pltpu.roll(t, FIELDS, 0) for t in swap] + [ghost]
        fresh = []
        for j, t in enumerate(tiles):
            beyond = jnp.where(up, turned[j], jnp.where(down, turned[j + 2], turned[j + 1]))
            west = jnp.where(cell == 0, 0.0, pltpu.roll(t, 1, 1))
            east = jnp.where(cell == PC - 1, 0.0, pltpu.roll(t, LANES - 1, 1))
            total = swap[j] + beyond + west + east - 4.0 * t
            fresh.append(t + nu[8 * j:8 * j + 8] * total)
        tiles = fresh
    return jnp.concatenate(tiles, axis=0)


def shards(mesh, fields, new_owner, leaflet, stiffness, coarse, coarse_of_slot, viscosity):
    n_ax, n_az = mesh.shape["axial"], mesh.shape["azim"]
    devices = n_ax * n_az
    patches, _, section = fields.shape
    records, rows, cols = leaflet.shape
    each = max(2, 3 * patches // (2 * devices))
    slots = devices * each
    wide = -(-slots // LANES) * LANES
    height = FIELDS * section // LANES
    view = fields.reshape(patches, FIELDS, section // LANES, LANES).transpose(0, 2, 1, 3)
    view = view.reshape(patches, height, LANES)
    vmem = pl.BlockSpec(memory_space=pltpu.VMEM)
    smem = pl.BlockSpec(memory_space=pltpu.SMEM)
    out = pl.pallas_call(
        functools.partial(send_kernel, n_ax, n_az, each),
        out_shape=jax.ShapeDtypeStruct((devices, each, height, LANES), F32),
        in_specs=[vmem, smem, smem, vmem, vmem, vmem, vmem],
        out_specs=pl.BlockSpec(memory_space=pl.ANY),
        scratch_shapes=[
            pltpu.VMEM((2, records, cols), F32),
            pltpu.VMEM((records, LANES), F32),
            pltpu.VMEM((2, records, cols), BF16),
            pltpu.VMEM((records, LANES), BF16),
            pltpu.VMEM((2, records, cols), BF16),
            pltpu.VMEM((2, records, LANES), BF16),
            pltpu.VMEM((rows // 8, 8 * records, cols), F32),
            pltpu.VMEM((patches + 1, height, LANES), BF16),
            pltpu.VMEM((devices, each, height, LANES), BF16),
            pltpu.VMEM((devices, each, height, LANES), BF16),
            pltpu.VMEM((devices, each, height, LANES), F32),
            pltpu.VMEM((coarse.shape[0], 2 * FIELDS, LANES), F32),
            pltpu.VMEM((1, wide), jnp.int32),
            pltpu.SMEM((1, wide), jnp.int32),
            pltpu.SemaphoreType.DMA((4,)),
            pltpu.SemaphoreType.DMA((4,)),
            pltpu.SemaphoreType.DMA((devices - 1,)),
            pltpu.SemaphoreType.DMA((devices - 1,)),
            pltpu.SemaphoreType.DMA((devices,)),
            pltpu.SemaphoreType.DMA,
        ],
        compiler_params=pltpu.CompilerParams(
            collective_id=0, has_side_effects=True, vmem_limit_bytes=28 << 20
        ),
        name="regrid",
    )(new_owner.reshape(1, patches), coarse_of_slot, viscosity, view, leaflet, stiffness, coarse)
    out = out.reshape(slots, section // LANES, FIELDS, LANES).transpose(0, 2, 1, 3)
    return out.reshape(slots, FIELDS, section)


def solution(mesh):
    placed = (
        P(("axial", "azim"), None, None),
        P(("axial", "azim"), None),
        P(None, "axial", "azim"),
        P(),
        P(("axial", "azim"), None),
        P(("axial", "azim")),
        P(),
    )
    return jax.shard_map(
        functools.partial(shards, mesh),
        mesh=mesh,
        in_specs=placed,
        out_specs=P(("axial", "azim"), None, None),
        check_vma=False,
    )
```

```python
import functools
import jax
import jax.numpy as jnp
from jax import lax
from jax.experimental import pallas as pl
from jax.experimental.pallas import tpu as pltpu
from jax.sharding import PartitionSpec as P

PC = 64
FIELDS = 4
STEPS = 2
SPREAD = 0.25
LANES = 128
MESH = pl.DeviceIdType.MESH
F32 = jnp.float32
BF16 = jnp.bfloat16


def iota(shape, dim):
    return lax.broadcasted_iota(jnp.int32, shape, dim)


def peer(i, n_ax, n_az):
    j = i // n_az
    da = lax.rem(n_ax // 2 + ((j + 1) // 2) * (1 - 2 * lax.rem(j, 2)), n_ax)
    return da, lax.rem(lax.rem(i, n_az) + 1, n_az)


def send_kernel(
    n_ax, n_az, each, owner_hbm, slot_hbm, nu_hbm, fields_hbm, leaf_hbm, stiff_hbm, coarse_hbm, out_ref,
    owner_ref, slot_ref, nu_ref, fields_ref, leaf_ref, stiff_ref, coarse_ref, load_sem,
    rows_f, cols_f, edge_rows, edge_cols, got_rows, got_cols, lap_ref, forced_ref, packed_ref,
    landed_ref, done_ref, strip_ref, pick_row, pick_ref,
    halo_send, halo_recv, send_sem, recv_sem, out_sem, pick_sem, closed_sem,
):
    a = lax.axis_index("axial")
    z = lax.axis_index("azim")
    me = a * n_az + z
    devices = n_ax * n_az
    records, rows, cols = leaf_ref.shape
    patches, height, _ = fields_ref.shape
    blocks = rows // 8

    pairs_in = (
        (leaf_hbm, leaf_ref), (stiff_hbm, stiff_ref), (owner_hbm, owner_ref), (coarse_hbm, coarse_ref),
        (slot_hbm, slot_ref), (nu_hbm, nu_ref), (fields_hbm, fields_ref),
    )
    loads = [
        pltpu.make_async_copy(src, dst, load_sem.at[i]) for i, (src, dst) in enumerate(pairs_in)
    ]
    for load in loads:
        load.start()
    got_rows[...] = jnp.zeros_like(got_rows)
    barrier = pltpu.get_barrier_semaphore()

    row_peers = [(a, lax.rem(z + dz, n_az)) for dz in range(1, n_az)]
    column_peers = [(lax.rem(a + da, n_ax), z) for da in range(1, n_ax)]
    for other in row_peers + column_peers:
        pl.semaphore_signal(barrier, inc=1, device_id=other, device_id_type=MESH)

    row_id = iota((rows, LANES), 0)
    lane_id = iota((rows, LANES), 1)
    eye_low = lane_id == row_id
    eye_high = lane_id == row_id + rows

    def edges(k, carry):
        x = leaf_ref[k].astype(F32)
        rows_f[0, pl.ds(k, 1), :] = x[0:1, :]
        rows_f[1, pl.ds(k, 1), :] = x[rows - 1:rows, :]
        first = jnp.broadcast_to(x[:, 0:1], (rows, LANES))
        last = jnp.broadcast_to(x[:, cols - 1:cols], (rows, LANES))
        both = jnp.where(eye_low, first, jnp.where(eye_high, last, 0.0))
        cols_f[pl.ds(k, 1), :] = jnp.sum(both, axis=0, keepdims=True)
        return carry

    loads[0].wait()
    lax.fori_loop(0, records, edges, 0, unroll=4)
    edge_rows[...] = rows_f[...].astype(BF16)
    edge_cols[...] = cols_f[...].astype(BF16)
    wide_row = iota((rows, cols), 0)
    wide_lane = iota((rows, cols), 1)

    def laplace(k, carry):
        x = leaf_ref[k].astype(F32)
        north = jnp.where(wide_row == 0, 0.0, pltpu.roll(x, 1, 0))
        south = jnp.where(wide_row == rows - 1, 0.0, pltpu.roll(x, rows - 1, 0))
        west = jnp.where(wide_lane == 0, 0.0, pltpu.roll(x, 1, 1))
        east = jnp.where(wide_lane == cols - 1, 0.0, pltpu.roll(x, cols - 1, 1))
        total = south + north + west + east - 4.0 * x
        for b in range(blocks):
            lap_ref[b, pl.ds(pl.multiple_of(k * 8, 8), 8), :] = total[b * 8:(b + 1) * 8, :]
        return carry

    lax.fori_loop(0, records // 2, laplace, 0, unroll=4)
    pl.semaphore_wait(barrier, len(row_peers) + len(column_peers))
    for other in row_peers:
        pl.semaphore_signal(closed_sem, inc=1, device_id=other, device_id_type=MESH)

    def halo(src, dst, i, device):
        return pltpu.make_async_remote_copy(
            src_ref=src, dst_ref=dst, send_sem=halo_send.at[i], recv_sem=halo_recv.at[i],
            device_id=device, device_id_type=MESH,
        )

    down = halo(edge_rows.at[1], got_rows.at[0], 0, (lax.rem(a + 1, n_ax), z))
    up = halo(edge_rows.at[0], got_rows.at[1], 1, (lax.rem(a + n_ax - 1, n_ax), z))
    right = halo(edge_cols, got_cols.at[0], 2, (a, lax.rem(z + 1, n_az)))
    left = halo(edge_cols, got_cols.at[1], 3, (a, lax.rem(z + n_az - 1, n_az)))

    @pl.when(a < n_ax - 1)
    def _():
        down.start()

    @pl.when(a > 0)
    def _():
        up.start()

    right.start()
    left.start()

    lax.fori_loop(records // 2, records, laplace, 0, unroll=4)
    for load in loads[1:6]:
        load.wait()
    pairs = records // FIELDS // 2
    width = pairs * FIELDS
    big = 8 * records
    out_row = iota((big, records), 0)
    record = iota((big, records), 1)
    within = lax.rem(out_row, width)
    wanted = lax.rem(within, FIELDS) * (2 * pairs) + 2 * (within // FIELDS) + out_row // (8 * width)
    row_pick = (record == wanted).astype(BF16)
    col_pick = (iota((records, big), 0) == iota((records, big), 1) // 8).astype(BF16)
    spread = jnp.dot(stiff_ref[...], col_pick, preferred_element_type=F32).astype(BF16)
    spread = jnp.dot(row_pick, spread, preferred_element_type=F32)
    same = lax.rem(iota((big, big), 0) // width, 8) == lax.rem(iota((big, big), 1), 8)
    law = jnp.where(same, spread, 0.0).astype(BF16)
    forced_ref[patches] = jnp.zeros(forced_ref.shape[1:], BF16)
    pick_slots(each, owner_ref, pick_row)
    picked = pltpu.make_async_copy(pick_row, pick_ref, pick_sem)
    picked.start()
    interpolate(coarse_ref, strip_ref)

    @pl.when(a > 0)
    def _():
        down.wait_recv()

    @pl.when(a < n_ax - 1)
    def _():
        up.wait_recv()

    right.wait_recv()
    left.wait_recv()
    rows_f2 = got_rows[...].astype(F32)
    cols_l = got_cols[0].astype(F32)
    cols_r = got_cols[1].astype(F32)

    @pl.when(a < n_ax - 1)
    def _():
        down.wait_send()

    @pl.when(a > 0)
    def _():
        up.wait_send()

    right.wait_send()
    left.wait_send()
    rows_f[...] = rows_f2
    cols_f[...] = jnp.where(iota(cols_l.shape, 1) < rows, cols_r, cols_l)
    first_row = iota((8, cols), 0) == 0
    last_row = iota((8, cols), 0) == 7
    first_lane = lane_id == 0
    last_lane = lane_id == LANES - 1

    def sides(k, carry):
        halo_cols = jnp.broadcast_to(cols_f[pl.ds(k, 1), :], (rows, LANES))
        after = jnp.sum(jnp.where(eye_low, halo_cols, 0.0), axis=1, keepdims=True)
        before = jnp.sum(jnp.where(eye_high, halo_cols, 0.0), axis=1, keepdims=True)
        west = jnp.where(first_lane, before, 0.0)
        east = jnp.where(last_lane, after, 0.0)
        here = pl.ds(pl.multiple_of(k * 8, 8), 8)
        lap_ref[0, here, :] += jnp.where(first_row, rows_f[0, pl.ds(k, 1), :], 0.0)
        lap_ref[blocks - 1, here, :] += jnp.where(last_row, rows_f[1, pl.ds(k, 1), :], 0.0)
        for b in range(blocks):
            lap_ref[b, here, :LANES] += west[b * 8:(b + 1) * 8]
            lap_ref[b, here, cols - LANES:] += east[b * 8:(b + 1) * 8]
        return carry

    lax.fori_loop(0, records, sides, 0, unroll=8)
    loads[6].wait()
    low = iota((width, LANES), 1) < PC
    across = cols // PC

    def force(b, carry):
        tension = jnp.dot(law, lap_ref[b].astype(BF16), preferred_element_type=F32)
        tension = tension.astype(BF16).astype(F32) * SPREAD
        for r in range(8):
            for t in range(cols // LANES):
                even = tension[r * width:(r + 1) * width, t * LANES:(t + 1) * LANES]
                odd = tension[(8 + r) * width:(9 + r) * width, t * LANES:(t + 1) * LANES]
                p = (b * 8 + r) * across + 2 * t
                first = jnp.where(low, even, pltpu.roll(odd, PC, 1))
                second = jnp.where(low, pltpu.roll(even, PC, 1), odd)
                forced_ref[p] = (fields_ref[p] + first).astype(BF16)
                forced_ref[p + 1] = (fields_ref[p + 1] + second).astype(BF16)
        return carry

    lax.fori_loop(0, blocks, force, 0)

    picked.wait()
    pl.semaphore_wait(closed_sem, len(row_peers))

    def outgoing(i):
        da, dz = peer(i, n_ax, n_az)
        ta, tz = lax.rem(a + da, n_ax), lax.rem(z + dz, n_az)
        other = ta * n_az + tz
        return other, pltpu.make_async_remote_copy(
            src_ref=packed_ref.at[other], dst_ref=landed_ref.at[me],
            send_sem=send_sem.at[i], recv_sem=recv_sem.at[i],
            device_id=(ta, tz), device_id_type=MESH,
        )

    def send(i, carry):
        other, copy = outgoing(i)
        for k in range(each):
            packed_ref[other, k] = forced_ref[pick_ref[0, other * each + k]]
        copy.start()
        return carry

    lax.fori_loop(0, devices - 1, send, 0)

    row = iota((height, LANES), 0)
    nu = jnp.full((height, LANES), nu_ref[0], F32)
    for f in range(1, FIELDS):
        nu = jnp.where(lax.rem(row, FIELDS) == f, nu_ref[f], nu)

    def written(source):
        return pltpu.make_async_copy(done_ref.at[source], out_ref.at[source], out_sem.at[source])

    for k in range(each):
        ghost = strip_ref[slot_ref[me * each + k]]
        block = forced_ref[pick_ref[0, me * each + k]].astype(F32)
        done_ref[me, k] = relax(block, ghost, nu)
    written(me).start()

    def arrive(i, carry):
        da, dz = peer(i, n_ax, n_az)
        source = lax.rem(a + n_ax - da, n_ax) * n_az + lax.rem(z + n_az - dz, n_az)
        pltpu.make_async_remote_copy(
            src_ref=packed_ref.at[source], dst_ref=landed_ref.at[source],
            send_sem=send_sem.at[i], recv_sem=recv_sem.at[i],
            device_id=(a, z), device_id_type=MESH,
        ).wait_recv()
        for k in range(each):
            ghost = strip_ref[slot_ref[source * each + k]]
            done_ref[source, k] = relax(landed_ref[source, k].astype(F32), ghost, nu)
        written(source).start()
        return carry

    lax.fori_loop(0, devices - 1, arrive, 0)

    def finish(i, carry):
        outgoing(i)[1].wait_send()
        written(i).wait()
        return carry

    lax.fori_loop(0, devices - 1, finish, 0)
    written(devices - 1).wait()


def pick_slots(each, owner_ref, pick_row):
    patches = owner_ref.shape[1]
    slots = pick_row.shape[1]
    square = (patches, patches)
    eye = iota(square, 0) == iota(square, 1)
    owner = owner_ref[...]
    across = jnp.broadcast_to(owner, square)
    along = jnp.sum(jnp.where(eye, across, 0), axis=1, keepdims=True)
    earlier = (along == across) & (iota(square, 0) < iota(square, 1))
    rank = jnp.sum(earlier.astype(jnp.int32), axis=0, keepdims=True)
    target = jnp.broadcast_to(owner * each + rank, square)
    target = jnp.sum(jnp.where(eye, target, 0), axis=1, keepdims=True)
    shape = (patches, slots)
    taken = target == iota(shape, 1)
    pick_row[...] = patches + jnp.sum(
        jnp.where(taken, iota(shape, 0) - patches, 0), axis=0, keepdims=True
    )


def interpolate(coarse_ref, strip_ref):
    fine = iota((PC, LANES), 1)
    src = iota((PC, LANES), 0)
    cell = lax.rem(fine, PC)
    near = (fine // PC) * (PC // 2) + cell // 2
    second = jnp.where(
        lax.rem(fine, 2) == 0,
        jnp.where(cell == 0, near, near - 1),
        jnp.where(cell == PC - 1, near, near + 1),
    )
    table = (0.75 * (src == near).astype(F32) + 0.25 * (src == second).astype(F32)).astype(BF16)
    for f in range(FIELDS):
        raw = coarse_ref[:, f * PC:(f + 1) * PC]
        top = raw.astype(BF16)
        rest = (raw - top.astype(F32)).astype(BF16)
        fine_cells = jnp.dot(top, table, preferred_element_type=F32)
        fine_cells = fine_cells + jnp.dot(rest, table, preferred_element_type=F32)
        strip_ref[:, f, :] = fine_cells
        strip_ref[:, FIELDS + f, :] = fine_cells


def relax(state, ghost, nu):
    shape = (8, LANES)
    lane = iota(shape, 1)
    low = iota(shape, 0) < FIELDS
    cell = lax.rem(lane, PC)
    up = (lane < PC) & low
    down = (lane >= PC) & (iota(shape, 0) >= FIELDS)
    count = state.shape[0] // 8
    tiles = [state[8 * j:8 * j + 8] for j in range(count)]
    for _ in range(STEPS):
        swap = [pltpu.roll(t, PC, 1) for t in tiles]
        turned = [ghost] + [pltpu.roll(t, FIELDS, 0) for t in swap] + [ghost]
        fresh = []
        for j, t in enumerate(tiles):
            beyond = jnp.where(up, turned[j], jnp.where(down, turned[j + 2], turned[j + 1]))
            west = jnp.where(cell == 0, 0.0, pltpu.roll(t, 1, 1))
            east = jnp.where(cell == PC - 1, 0.0, pltpu.roll(t, LANES - 1, 1))
            total = swap[j] + beyond + west + east - 4.0 * t
            fresh.append(t + nu[8 * j:8 * j + 8] * total)
        tiles = fresh
    return jnp.concatenate(tiles, axis=0)


def shards(mesh, fields, new_owner, leaflet, stiffness, coarse, coarse_of_slot, viscosity):
    n_ax, n_az = mesh.shape["axial"], mesh.shape["azim"]
    devices = n_ax * n_az
    patches, _, section = fields.shape
    records, rows, cols = leaflet.shape
    each = max(2, 3 * patches // (2 * devices))
    slots = devices * each
    wide = -(-slots // LANES) * LANES
    height = FIELDS * section // LANES
    view = fields.reshape(patches, FIELDS, section // LANES, LANES).transpose(0, 2, 1, 3)
    view = view.reshape(patches, height, LANES)
    out = pl.pallas_call(
        functools.partial(send_kernel, n_ax, n_az, each),
        out_shape=jax.ShapeDtypeStruct((devices, each, height, LANES), F32),
        in_specs=[pl.BlockSpec(memory_space=pltpu.HBM)] * 7,
        out_specs=pl.BlockSpec(memory_space=pl.ANY),
        scratch_shapes=[
            pltpu.VMEM((1, patches), jnp.int32),
            pltpu.SMEM((slots,), jnp.int32),
            pltpu.SMEM((FIELDS,), F32),
            pltpu.VMEM((patches, height, LANES), F32),
            pltpu.VMEM(leaflet.shape, BF16),
            pltpu.VMEM(stiffness.shape, BF16),
            pltpu.VMEM(coarse.shape, F32),
            pltpu.SemaphoreType.DMA((7,)),
            pltpu.VMEM((2, records, cols), F32),
            pltpu.VMEM((records, LANES), F32),
            pltpu.VMEM((2, records, cols), BF16),
            pltpu.VMEM((records, LANES), BF16),
            pltpu.VMEM((2, records, cols), BF16),
            pltpu.VMEM((2, records, LANES), BF16),
            pltpu.VMEM((rows // 8, 8 * records, cols), F32),
            pltpu.VMEM((patches + 1, height, LANES), BF16),
            pltpu.VMEM((devices, each, height, LANES), BF16),
            pltpu.VMEM((devices, each, height, LANES), BF16),
            pltpu.VMEM((devices, each, height, LANES), F32),
            pltpu.VMEM((coarse.shape[0], 2 * FIELDS, LANES), F32),
            pltpu.VMEM((1, wide), jnp.int32),
            pltpu.SMEM((1, wide), jnp.int32),
            pltpu.SemaphoreType.DMA((4,)),
            pltpu.SemaphoreType.DMA((4,)),
            pltpu.SemaphoreType.DMA((devices - 1,)),
            pltpu.SemaphoreType.DMA((devices - 1,)),
            pltpu.SemaphoreType.DMA((devices,)),
            pltpu.SemaphoreType.DMA,
            pltpu.SemaphoreType.REGULAR,
        ],
        compiler_params=pltpu.CompilerParams(
            collective_id=0, has_side_effects=True, vmem_limit_bytes=62 << 20
        ),
        name="regrid",
    )(new_owner.reshape(1, patches), coarse_of_slot, viscosity, view, leaflet, stiffness, coarse)
    out = out.reshape(slots, section // LANES, FIELDS, LANES).transpose(0, 2, 1, 3)
    return out.reshape(slots, FIELDS, section)


def solution(mesh):
    placed = (
        P(("axial", "azim"), None, None),
        P(("axial", "azim"), None),
        P(None, "axial", "azim"),
        P(),
        P(("axial", "azim"), None),
        P(("axial", "azim")),
        P(),
    )
    return jax.shard_map(
        functools.partial(shards, mesh),
        mesh=mesh,
        in_specs=placed,
        out_specs=P(("axial", "azim"), None, None),
        check_vma=False,
    )
```

```python
import functools
import jax
import jax.numpy as jnp
from jax import lax
from jax.experimental import pallas as pl
from jax.experimental.pallas import tpu as pltpu
from jax.sharding import PartitionSpec as P

PC = 64
FIELDS = 4
STEPS = 2
SPREAD = 0.25
LANES = 128
MESH = pl.DeviceIdType.MESH
F32 = jnp.float32
BF16 = jnp.bfloat16


def iota(shape, dim):
    return lax.broadcasted_iota(jnp.int32, shape, dim)


def peer(i, n_ax, n_az):
    j = i // n_az
    da = lax.rem(n_ax // 2 + ((j + 1) // 2) * (1 - 2 * lax.rem(j, 2)), n_ax)
    return da, lax.rem(lax.rem(i, n_az) + 1, n_az)


def send_kernel(
    n_ax, n_az, each, owner_hbm, slot_hbm, nu_hbm, fields_hbm, leaf_hbm, stiff_hbm, coarse_hbm, out_ref,
    owner_ref, slot_ref, nu_ref, fields_ref, leaf_ref, stiff_ref, coarse_ref, load_sem,
    rows_f, cols_f, edge_rows, edge_cols, got_rows, got_cols, lap_ref, forced_ref, packed_ref,
    landed_ref, done_ref, strip_ref, pick_row, pick_ref,
    halo_send, halo_recv, send_sem, recv_sem, out_sem, pick_sem, closed_sem,
):
    a = lax.axis_index("axial")
    z = lax.axis_index("azim")
    me = a * n_az + z
    devices = n_ax * n_az
    records, rows, cols = leaf_ref.shape
    patches, height, _ = fields_ref.shape
    blocks = rows // 8

    pairs_in = (
        (leaf_hbm, leaf_ref), (stiff_hbm, stiff_ref), (owner_hbm, owner_ref), (coarse_hbm, coarse_ref),
        (slot_hbm, slot_ref), (nu_hbm, nu_ref), (fields_hbm, fields_ref),
    )
    loads = [
        pltpu.make_async_copy(src, dst, load_sem.at[i]) for i, (src, dst) in enumerate(pairs_in)
    ]
    for load in loads:
        load.start()
    got_rows[...] = jnp.zeros_like(got_rows)
    barrier = pltpu.get_barrier_semaphore()

    row_peers = [(a, lax.rem(z + dz, n_az)) for dz in range(1, n_az)]
    column_peers = [(lax.rem(a + da, n_ax), z) for da in range(1, n_ax)]
    for other in row_peers + column_peers:
        pl.semaphore_signal(barrier, inc=1, device_id=other, device_id_type=MESH)

    row_id = iota((rows, LANES), 0)
    lane_id = iota((rows, LANES), 1)
    eye_low = lane_id == row_id
    eye_high = lane_id == row_id + rows

    def edges(k, carry):
        x = leaf_ref[k].astype(F32)
        rows_f[0, pl.ds(k, 1), :] = x[0:1, :]
        rows_f[1, pl.ds(k, 1), :] = x[rows - 1:rows, :]
        first = jnp.broadcast_to(x[:, 0:1], (rows, LANES))
        last = jnp.broadcast_to(x[:, cols - 1:cols], (rows, LANES))
        both = jnp.where(eye_low, first, jnp.where(eye_high, last, 0.0))
        cols_f[pl.ds(k, 1), :] = jnp.sum(both, axis=0, keepdims=True)
        return carry

    loads[0].wait()
    lax.fori_loop(0, records, edges, 0, unroll=4)
    edge_rows[...] = rows_f[...].astype(BF16)
    edge_cols[...] = cols_f[...].astype(BF16)
    wide_row = iota((rows, cols), 0)
    wide_lane = iota((rows, cols), 1)

    def laplace(k, carry):
        x = leaf_ref[k].astype(F32)
        north = jnp.where(wide_row == 0, 0.0, pltpu.roll(x, 1, 0))
        south = jnp.where(wide_row == rows - 1, 0.0, pltpu.roll(x, rows - 1, 0))
        west = jnp.where(wide_lane == 0, 0.0, pltpu.roll(x, 1, 1))
        east = jnp.where(wide_lane == cols - 1, 0.0, pltpu.roll(x, cols - 1, 1))
        total = south + north + west + east - 4.0 * x
        for b in range(blocks):
            lap_ref[b, pl.ds(pl.multiple_of(k * 8, 8), 8), :] = total[b * 8:(b + 1) * 8, :]
        return carry

    lax.fori_loop(0, records // 2, laplace, 0, unroll=4)
    pl.semaphore_wait(barrier, len(row_peers) + len(column_peers))
    for other in row_peers:
        pl.semaphore_signal(closed_sem, inc=1, device_id=other, device_id_type=MESH)

    def halo(src, dst, i, device):
        return pltpu.make_async_remote_copy(
            src_ref=src, dst_ref=dst, send_sem=halo_send.at[i], recv_sem=halo_recv.at[i],
            device_id=device, device_id_type=MESH,
        )

    down = halo(edge_rows.at[1], got_rows.at[0], 0, (lax.rem(a + 1, n_ax), z))
    up = halo(edge_rows.at[0], got_rows.at[1], 1, (lax.rem(a + n_ax - 1, n_ax), z))
    right = halo(edge_cols, got_cols.at[0], 2, (a, lax.rem(z + 1, n_az)))
    left = halo(edge_cols, got_cols.at[1], 3, (a, lax.rem(z + n_az - 1, n_az)))

    @pl.when(a < n_ax - 1)
    def _():
        down.start()

    @pl.when(a > 0)
    def _():
        up.start()

    right.start()
    left.start()

    lax.fori_loop(records // 2, records, laplace, 0, unroll=4)
    for load in loads[1:6]:
        load.wait()
    pairs = records // FIELDS // 2
    width = pairs * FIELDS
    big = 8 * records
    out_row = iota((big, records), 0)
    record = iota((big, records), 1)
    within = lax.rem(out_row, width)
    wanted = lax.rem(within, FIELDS) * (2 * pairs) + 2 * (within // FIELDS) + out_row // (8 * width)
    row_pick = (record == wanted).astype(BF16)
    col_pick = (iota((records, big), 0) == iota((records, big), 1) // 8).astype(BF16)
    spread = jnp.dot(stiff_ref[...], col_pick, preferred_element_type=F32).astype(BF16)
    spread = jnp.dot(row_pick, spread, preferred_element_type=F32)
    same = lax.rem(iota((big, big), 0) // width, 8) == lax.rem(iota((big, big), 1), 8)
    law = jnp.where(same, spread, 0.0).astype(BF16)
    forced_ref[patches] = jnp.zeros(forced_ref.shape[1:], BF16)
    pick_slots(each, owner_ref, pick_row)
    picked = pltpu.make_async_copy(pick_row, pick_ref, pick_sem)
    picked.start()
    interpolate(coarse_ref, strip_ref)

    @pl.when(a > 0)
    def _():
        down.wait_recv()

    @pl.when(a < n_ax - 1)
    def _():
        up.wait_recv()

    right.wait_recv()
    left.wait_recv()
    rows_f2 = got_rows[...].astype(F32)
    cols_l = got_cols[0].astype(F32)
    cols_r = got_cols[1].astype(F32)

    @pl.when(a < n_ax - 1)
    def _():
        down.wait_send()

    @pl.when(a > 0)
    def _():
        up.wait_send()

    right.wait_send()
    left.wait_send()
    rows_f[...] = rows_f2
    cols_f[...] = jnp.where(iota(cols_l.shape, 1) < rows, cols_r, cols_l)
    first_row = iota((8, cols), 0) == 0
    last_row = iota((8, cols), 0) == 7
    first_lane = lane_id == 0
    last_lane = lane_id == LANES - 1

    def sides(k, carry):
        halo_cols = jnp.broadcast_to(cols_f[pl.ds(k, 1), :], (rows, LANES))
        after = jnp.sum(jnp.where(eye_low, halo_cols, 0.0), axis=1, keepdims=True)
        before = jnp.sum(jnp.where(eye_high, halo_cols, 0.0), axis=1, keepdims=True)
        west = jnp.where(first_lane, before, 0.0)
        east = jnp.where(last_lane, after, 0.0)
        here = pl.ds(pl.multiple_of(k * 8, 8), 8)
        lap_ref[0, here, :] += jnp.where(first_row, rows_f[0, pl.ds(k, 1), :], 0.0)
        lap_ref[blocks - 1, here, :] += jnp.where(last_row, rows_f[1, pl.ds(k, 1), :], 0.0)
        for b in range(blocks):
            lap_ref[b, here, :LANES] += west[b * 8:(b + 1) * 8]
            lap_ref[b, here, cols - LANES:] += east[b * 8:(b + 1) * 8]
        return carry

    lax.fori_loop(0, records, sides, 0, unroll=8)
    loads[6].wait()
    low = iota((width, LANES), 1) < PC
    across = cols // PC

    def force(b, carry):
        tension = jnp.dot(law, lap_ref[b].astype(BF16), preferred_element_type=F32)
        tension = tension.astype(BF16).astype(F32) * SPREAD
        for r in range(8):
            for t in range(cols // LANES):
                even = tension[r * width:(r + 1) * width, t * LANES:(t + 1) * LANES]
                odd = tension[(8 + r) * width:(9 + r) * width, t * LANES:(t + 1) * LANES]
                p = (b * 8 + r) * across + 2 * t
                first = jnp.where(low, even, pltpu.roll(odd, PC, 1))
                second = jnp.where(low, pltpu.roll(even, PC, 1), odd)
                forced_ref[p] = (fields_ref[p] + first).astype(BF16)
                forced_ref[p + 1] = (fields_ref[p + 1] + second).astype(BF16)
        return carry

    lax.fori_loop(0, blocks, force, 0)

    picked.wait()
    pl.semaphore_wait(closed_sem, len(row_peers))

    def outgoing(i):
        da, dz = peer(i, n_ax, n_az)
        ta, tz = lax.rem(a + da, n_ax), lax.rem(z + dz, n_az)
        other = ta * n_az + tz
        return other, pltpu.make_async_remote_copy(
            src_ref=packed_ref.at[other], dst_ref=landed_ref.at[me],
            send_sem=send_sem.at[i], recv_sem=recv_sem.at[i],
            device_id=(ta, tz), device_id_type=MESH,
        )

    def send(i, carry):
        other, copy = outgoing(i)
        for k in range(each):
            packed_ref[other, k] = forced_ref[pick_ref[0, other * each + k]]
        copy.start()
        return carry

    lax.fori_loop(0, devices - 1, send, 0)

    row = iota((height, LANES), 0)
    nu = jnp.full((height, LANES), nu_ref[0], F32)
    for f in range(1, FIELDS):
        nu = jnp.where(lax.rem(row, FIELDS) == f, nu_ref[f], nu)

    def written(source):
        return pltpu.make_async_copy(done_ref.at[source], out_ref.at[source], out_sem.at[source])

    for k in range(each):
        ghost = strip_ref[slot_ref[me * each + k]]
        block = forced_ref[pick_ref[0, me * each + k]].astype(F32)
        done_ref[me, k] = relax(block, ghost, nu)
    written(me).start()

    def arrive(turn, carry):
        i = lax.rem(turn + devices - n_az, devices - 1)
        da, dz = peer(i, n_ax, n_az)
        source = lax.rem(a + n_ax - da, n_ax) * n_az + lax.rem(z + n_az - dz, n_az)
        pltpu.make_async_remote_copy(
            src_ref=packed_ref.at[source], dst_ref=landed_ref.at[source],
            send_sem=send_sem.at[i], recv_sem=recv_sem.at[i],
            device_id=(a, z), device_id_type=MESH,
        ).wait_recv()
        for k in range(each):
            ghost = strip_ref[slot_ref[source * each + k]]
            done_ref[source, k] = relax(landed_ref[source, k].astype(F32), ghost, nu)
        written(source).start()
        return carry

    lax.fori_loop(0, devices - 1, arrive, 0)

    def finish(i, carry):
        outgoing(i)[1].wait_send()
        written(i).wait()
        return carry

    lax.fori_loop(0, devices - 1, finish, 0)
    written(devices - 1).wait()


def pick_slots(each, owner_ref, pick_row):
    patches = owner_ref.shape[1]
    slots = pick_row.shape[1]
    square = (patches, patches)
    eye = iota(square, 0) == iota(square, 1)
    owner = owner_ref[...]
    across = jnp.broadcast_to(owner, square)
    along = jnp.sum(jnp.where(eye, across, 0), axis=1, keepdims=True)
    earlier = (along == across) & (iota(square, 0) < iota(square, 1))
    rank = jnp.sum(earlier.astype(jnp.int32), axis=0, keepdims=True)
    target = jnp.broadcast_to(owner * each + rank, square)
    target = jnp.sum(jnp.where(eye, target, 0), axis=1, keepdims=True)
    shape = (patches, slots)
    taken = target == iota(shape, 1)
    pick_row[...] = patches + jnp.sum(
        jnp.where(taken, iota(shape, 0) - patches, 0), axis=0, keepdims=True
    )


def interpolate(coarse_ref, strip_ref):
    fine = iota((PC, LANES), 1)
    src = iota((PC, LANES), 0)
    cell = lax.rem(fine, PC)
    near = (fine // PC) * (PC // 2) + cell // 2
    second = jnp.where(
        lax.rem(fine, 2) == 0,
        jnp.where(cell == 0, near, near - 1),
        jnp.where(cell == PC - 1, near, near + 1),
    )
    table = (0.75 * (src == near).astype(F32) + 0.25 * (src == second).astype(F32)).astype(BF16)
    for f in range(FIELDS):
        raw = coarse_ref[:, f * PC:(f + 1) * PC]
        top = raw.astype(BF16)
        rest = (raw - top.astype(F32)).astype(BF16)
        fine_cells = jnp.dot(top, table, preferred_element_type=F32)
        fine_cells = fine_cells + jnp.dot(rest, table, preferred_element_type=F32)
        strip_ref[:, f, :] = fine_cells
        strip_ref[:, FIELDS + f, :] = fine_cells


def relax(state, ghost, nu):
    shape = (8, LANES)
    lane = iota(shape, 1)
    low = iota(shape, 0) < FIELDS
    cell = lax.rem(lane, PC)
    up = (lane < PC) & low
    down = (lane >= PC) & (iota(shape, 0) >= FIELDS)
    count = state.shape[0] // 8
    tiles = [state[8 * j:8 * j + 8] for j in range(count)]
    for _ in range(STEPS):
        swap = [pltpu.roll(t, PC, 1) for t in tiles]
        turned = [ghost] + [pltpu.roll(t, FIELDS, 0) for t in swap] + [ghost]
        fresh = []
        for j, t in enumerate(tiles):
            beyond = jnp.where(up, turned[j], jnp.where(down, turned[j + 2], turned[j + 1]))
            west = jnp.where(cell == 0, 0.0, pltpu.roll(t, 1, 1))
            east = jnp.where(cell == PC - 1, 0.0, pltpu.roll(t, LANES - 1, 1))
            total = swap[j] + beyond + west + east - 4.0 * t
            fresh.append(t + nu[8 * j:8 * j + 8] * total)
        tiles = fresh
    return jnp.concatenate(tiles, axis=0)


def shards(mesh, fields, new_owner, leaflet, stiffness, coarse, coarse_of_slot, viscosity):
    n_ax, n_az = mesh.shape["axial"], mesh.shape["azim"]
    devices = n_ax * n_az
    patches, _, section = fields.shape
    records, rows, cols = leaflet.shape
    each = max(2, 3 * patches // (2 * devices))
    slots = devices * each
    wide = -(-slots // LANES) * LANES
    height = FIELDS * section // LANES
    view = fields.reshape(patches, FIELDS, section // LANES, LANES).transpose(0, 2, 1, 3)
    view = view.reshape(patches, height, LANES)
    out = pl.pallas_call(
        functools.partial(send_kernel, n_ax, n_az, each),
        out_shape=jax.ShapeDtypeStruct((devices, each, height, LANES), F32),
        in_specs=[pl.BlockSpec(memory_space=pltpu.HBM)] * 7,
        out_specs=pl.BlockSpec(memory_space=pl.ANY),
        scratch_shapes=[
            pltpu.VMEM((1, patches), jnp.int32),
            pltpu.SMEM((slots,), jnp.int32),
            pltpu.SMEM((FIELDS,), F32),
            pltpu.VMEM((patches, height, LANES), F32),
            pltpu.VMEM(leaflet.shape, BF16),
            pltpu.VMEM(stiffness.shape, BF16),
            pltpu.VMEM(coarse.shape, F32),
            pltpu.SemaphoreType.DMA((7,)),
            pltpu.VMEM((2, records, cols), F32),
            pltpu.VMEM((records, LANES), F32),
            pltpu.VMEM((2, records, cols), BF16),
            pltpu.VMEM((records, LANES), BF16),
            pltpu.VMEM((2, records, cols), BF16),
            pltpu.VMEM((2, records, LANES), BF16),
            pltpu.VMEM((rows // 8, 8 * records, cols), F32),
            pltpu.VMEM((patches + 1, height, LANES), BF16),
            pltpu.VMEM((devices, each, height, LANES), BF16),
            pltpu.VMEM((devices, each, height, LANES), BF16),
            pltpu.VMEM((devices, each, height, LANES), F32),
            pltpu.VMEM((coarse.shape[0], 2 * FIELDS, LANES), F32),
            pltpu.VMEM((1, wide), jnp.int32),
            pltpu.SMEM((1, wide), jnp.int32),
            pltpu.SemaphoreType.DMA((4,)),
            pltpu.SemaphoreType.DMA((4,)),
            pltpu.SemaphoreType.DMA((devices - 1,)),
            pltpu.SemaphoreType.DMA((devices - 1,)),
            pltpu.SemaphoreType.DMA((devices,)),
            pltpu.SemaphoreType.DMA,
            pltpu.SemaphoreType.REGULAR,
        ],
        compiler_params=pltpu.CompilerParams(
            collective_id=0, has_side_effects=True, vmem_limit_bytes=62 << 20
        ),
        name="regrid",
    )(new_owner.reshape(1, patches), coarse_of_slot, viscosity, view, leaflet, stiffness, coarse)
    out = out.reshape(slots, section // LANES, FIELDS, LANES).transpose(0, 2, 1, 3)
    return out.reshape(slots, FIELDS, section)


def solution(mesh):
    placed = (
        P(("axial", "azim"), None, None),
        P(("axial", "azim"), None),
        P(None, "axial", "azim"),
        P(),
        P(("axial", "azim"), None),
        P(("axial", "azim")),
        P(),
    )
    return jax.shard_map(
        functools.partial(shards, mesh),
        mesh=mesh,
        in_specs=placed,
        out_specs=P(("axial", "azim"), None, None),
        check_vma=False,
    )
```
